32 devices in a mesh: gx: 2 (over x), gy: 4 (over z), gz: 4 (over y, core).
Axes of the slice: x: 2, y: 2, z: 4, core: 2. Of those that a mesh axis runs over, the one named last changes fastest.
Arguments:
- local_displacement: float32 [2, 4, 4, 6, 128, 128], P('gx', 'gy', 'gz'), may hold values from -6 to 6
- coarse_load: float32 [2, 4, 4, 6, 128], P('gx', 'gy', 'gz'), may hold values from -12 to 12
- flexibility: float32 [2, 4, 4, 768, 768], P('gx', 'gy', 'gz'), as said below
- block_map: int32 [2, 4, 4, 768], P('gx', 'gy', 'gz'), may hold values from 0 to 767, each once within a row
- mode_counts: int32 [2, 4, 4], P('gx', 'gy', 'gz'), may hold values from 3 to 6, as said below
- mode_traces: float32 [2, 4, 4, 6, 6, 128], P('gx', 'gy', 'gz')
- coarse_rows: float32 [2, 4, 4, 6, 192], P('gx', 'gy', 'gz'), as said below
- stored_dirs: float32 [2, 4, 4, 40, 6, 128], P('gx', 'gy', 'gz'), as said below
- stored_images: float32 [2, 4, 4, 40, 6, 128], P('gx', 'gy', 'gz'), as said below
- stored_curv: float32 [40], replicated, may hold values from 1 to 4
Outputs:
- multipliers: float32 [2, 4, 4, 6, 128, 128], P('gx', 'gy', 'gz')
- residual: float32 [2, 4, 4, 6, 128, 128], P('gx', 'gy', 'gz')
The draws below stay inside these ranges and needn't reach their ends.
Inputs may be any that keep to these rules, and one draw needn't show every extreme that they name: `flexibility`: each subdomain's matrix is symmetric positive definite. `coarse_rows`: read as a [192, 192] matrix it is exactly symmetric: the inverse of G^T G for the coarse basis G of the present modes, with ones added on the diagonal of absent modes. `mode_counts`: modes numbered from the count on are absent. `block_map`: each subdomain's row names every interface position once. `stored_dirs`: both copies of every face agree: slot 2a of a subdomain equals slot 2a+1 of its lower neighbour along grid dimension a. `stored_images`: both copies of every face agree: slot 2a of a subdomain equals slot 2a+1 of its lower neighbour along grid dimension a.
All inputs are finite; a program needn't handle non-finite values.
Results may differ from the reference program's by a relative error of at most 0.0003.
Values sent between devices are 32-bit elements; how exact they have to be, the bound alone decides.
A program may use at most 128 MiB of HBM per device.

```python
import math
import jax
import jax.numpy as jnp
from jax import lax

FACE = 128
RHS = 128
STORED = 40
RM = 6
ITERS = 3
NB = 768
SX = 2
SY = 4
SZ = 4
SUBS = 32
CMODES = 192


def face_draw(draw_key, shape):
    return jax.random.normal(draw_key, shape, jnp.float32)


def coarse_bundle(key):
    counts = jax.random.randint(jax.random.fold_in(key, 101), (SX, SY, SZ), 3, RM + 1, dtype=jnp.int32)
    shared = face_draw(jax.random.fold_in(key, 102), (SX, SY, SZ, RM, 3, FACE))
    own_part = face_draw(jax.random.fold_in(key, 103), (SX, SY, SZ, RM, 6, FACE))
    slots = []
    for grid_dim in range(3):
        plus_face = shared[:, :, :, :, grid_dim]
        slots.append(jnp.roll(plus_face, 1, axis=grid_dim))
        slots.append(plus_face)
    traces = (jnp.stack(slots, axis=4) + 0.25 * own_part) * FACE ** (-0.5)
    present = (jnp.arange(RM, dtype=jnp.int32)[None, None, None, :] < counts[..., None]).astype(jnp.float32)
    masked = traces * present[..., None, None]
    diagonal_blocks = jnp.einsum('xyzmsf,xyznsf->xyzmn', masked, masked).reshape(SUBS, RM, RM)
    unit = jnp.eye(SUBS, dtype=jnp.float32)
    gram = jnp.einsum('st,smn->smtn', unit, diagonal_blocks)
    for grid_dim in range(3):
        above = jnp.roll(masked[:, :, :, :, 2 * grid_dim], -1, axis=grid_dim)
        coupling = -jnp.einsum('xyzmf,xyznf->xyzmn', masked[:, :, :, :, 2 * grid_dim + 1], above).reshape(SUBS, RM, RM)
        shifter = jnp.roll(unit.reshape(SX, SY, SZ, SUBS), -1, axis=grid_dim).reshape(SUBS, SUBS)
        gram = gram + jnp.einsum('st,smn->smtn', shifter, coupling) + jnp.einsum('st,smn->tnsm', shifter, coupling)
    absent = (1.0 - present).reshape(CMODES)
    matrix = gram.reshape(CMODES, CMODES) + jnp.diag(absent)
    inverse = jnp.linalg.inv(matrix)
    inverse = 0.5 * (inverse + inverse.T)
    return (counts, traces, inverse.reshape(SX, SY, SZ, RM, CMODES))


def draw_mode_counts(key, part):
    return coarse_bundle(key)[0]


def draw_mode_traces(key, part):
    return coarse_bundle(key)[1]


def draw_coarse_rows(key, part):
    return coarse_bundle(key)[2]


def stored_slabs(key, salt, spread):
    raw_key = jax.random.fold_in(key, salt)
    owned = jax.random.normal(raw_key, (SX, SY, SZ, STORED, 3, FACE), jnp.float32) * spread
    slots = []
    for grid_dim in range(3):
        plus_face = owned[:, :, :, :, grid_dim]
        slots.append(jnp.roll(plus_face, 1, axis=grid_dim))
        slots.append(plus_face)
    return jnp.stack(slots, axis=4)


def draw_stored_dirs(key, part):
    return stored_slabs(key, 201, 0.1)


def draw_stored_images(key, part):
    return stored_slabs(key, 202, (3.0 * FACE * SUBS) ** (-0.5))


def draw_flexibility(key, part):
    raw_key = jax.random.fold_in(key, 301)
    raw = jax.random.normal(raw_key, (SX, SY, SZ, NB, NB), jnp.float32)
    symmetric = (raw + jnp.swapaxes(raw, -1, -2)) * (0.35 / (2.0 * NB) ** 0.5)
    scales = jnp.exp(jax.random.uniform(jax.random.fold_in(key, 302), (SX, SY, SZ, NB), jnp.float32, jnp.log(0.7), jnp.log(1.4)))
    core = symmetric + jnp.eye(NB, dtype=jnp.float32)
    return core * (scales[..., :, None] * scales[..., None, :])


def block_levels(own_key, dims, pieces, low, high):
    gain, own = 1.0, jax.random.fold_in(own_key, 6)
    for dim, parts in pieces:
        draws = jnp.exp(jax.random.uniform(jax.random.fold_in(own, dim), (parts,), jnp.float32, low / len(pieces), high / len(pieces)))
        gain = gain * jnp.repeat(draws, dims[dim] // parts).reshape([-1 if axis == dim else 1 for axis in range(len(dims))])
    return gain


def normal_values(rng, extent, scale, most, shards=(), held_as=jnp.bfloat16):
    values = jax.random.normal(rng, extent, jnp.float32) * scale
    if len(shards) > 0:
        values = block_levels(rng, extent, shards, -0.22, 0.18) * values
    return jnp.clip(values, min=-most, max=most).astype(held_as)


def setup_inputs(seed: int = 0) -> dict:
    key_list = jax.random.split(jax.random.key(seed), 11)
    local_displacement = normal_values(key_list[0], (SX, SY, SZ, 6, FACE, RHS), 1.0, 6.0, ((0, 2), (1, 4), (2, 4)), jnp.float32)
    coarse_load = normal_values(key_list[1], (SX, SY, SZ, RM, RHS), 2.0, 12.0, ((0, 2), (1, 4), (2, 4)), jnp.float32)
    flexibility = draw_flexibility(jax.random.fold_in(key_list[10], 71), 0)
    block_map = jax.vmap(lambda own: jax.random.permutation(own, NB))(jax.random.split(key_list[3], SX * SY * SZ)).reshape((SX, SY, SZ, NB)).astype(jnp.int32)
    mode_counts = draw_mode_counts(jax.random.fold_in(key_list[10], 71), 0)
    mode_traces = draw_mode_traces(jax.random.fold_in(key_list[10], 71), 0)
    coarse_rows = draw_coarse_rows(jax.random.fold_in(key_list[10], 71), 0)
    stored_dirs = draw_stored_dirs(jax.random.fold_in(key_list[10], 71), 0)
    stored_images = draw_stored_images(jax.random.fold_in(key_list[10], 71), 0)
    stored_curv = jnp.clip(jnp.exp(jax.random.uniform(key_list[9], (STORED,), jnp.float32, math.log(1.0), math.log(4.0))), 1.0, 4.0)
    return {"local_displacement": local_displacement, "coarse_load": coarse_load, "flexibility": flexibility, "block_map": block_map, "mode_counts": mode_counts, "mode_traces": mode_traces, "coarse_rows": coarse_rows, "stored_dirs": stored_dirs, "stored_images": stored_images, "stored_curv": stored_curv}


precise = lax.Precision.HIGHEST

def assemble(field):
    slots = []
    for grid_dim in range(3):
        minus_side = field[:, :, :, 2 * grid_dim]
        plus_side = field[:, :, :, 2 * grid_dim + 1]
        slots.append(minus_side + jnp.roll(plus_side, 1, axis=grid_dim))
        slots.append(plus_side + jnp.roll(minus_side, -1, axis=grid_dim))
    return jnp.stack(slots, axis=3)

def single_apply(matrix, mapping, vector):
    picked = vector[mapping]
    product = jnp.dot(matrix, picked, precision=precise)
    return jnp.zeros_like(vector).at[mapping].set(product)

def flex_apply(flexibility, block_map, field):
    flat = field.reshape(SUBS, NB, RHS)
    result = jax.vmap(single_apply)(flexibility.reshape(SUBS, NB, NB), block_map.reshape(SUBS, NB), flat)
    return result.reshape(field.shape)

def coarse_solve(coarse_rows, loads):
    matrix = coarse_rows.reshape(CMODES, CMODES)
    return jnp.dot(matrix, loads.reshape(CMODES, RHS), precision=precise).reshape(SX, SY, SZ, RM, RHS)

def graph(signed, alpha):
    return assemble(jnp.einsum('xyzmsf,xyzmr->xyzsfr', signed, alpha, precision=precise))

def inner(first, second):
    return jnp.sum(first[:, :, :, 1::2] * second[:, :, :, 1::2], axis=(0, 1, 2, 3, 4))

def reference(local_displacement, coarse_load, flexibility, block_map, mode_counts, mode_traces, coarse_rows, stored_dirs, stored_images, stored_curv):
    signs = jnp.array([-1.0, 1.0, -1.0, 1.0, -1.0, 1.0], jnp.float32)
    field_signs = signs[:, None, None]
    present = (jnp.arange(RM, dtype=jnp.int32)[None, None, None, :] < mode_counts[..., None]).astype(jnp.float32)
    signed = mode_traces * present[..., None, None] * signs[:, None]

    def project(field):
        partial_loads = jnp.einsum('xyzmsf,xyzsfr->xyzmr', signed, field, precision=precise)
        return field - graph(signed, coarse_solve(coarse_rows, partial_loads))
    lam = graph(signed, coarse_solve(coarse_rows, coarse_load))
    moved = flex_apply(flexibility, block_map, field_signs * lam)
    resid = project(assemble(field_signs * (local_displacement - moved)))
    directions, images, curves = ([], [], [])
    for step in range(ITERS):
        stored_part = jnp.einsum('xyzisf,xyzsfr->ir', stored_images[:, :, :, :, 1::2], resid[:, :, :, 1::2], precision=precise)
        beta = stored_part / stored_curv[:, None]
        gammas = [inner(images[index], resid) / curves[index] for index in range(len(images))]
        direction = resid - jnp.einsum('xyzisf,ir->xyzsfr', stored_dirs, beta, precision=precise)
        for index in range(len(directions)):
            direction = direction - directions[index] * gammas[index]
        image_now = project(assemble(field_signs * flex_apply(flexibility, block_map, field_signs * direction)))
        curve = inner(direction, image_now)
        rate = inner(direction, resid) / curve
        lam = lam + rate * direction
        resid = resid - rate * image_now
        directions.append(direction)
        images.append(image_now)
        curves.append(curve)
    return (lam, resid)
```

```python
import functools

import jax
import jax.numpy as jnp
from jax import lax
from jax.experimental import pallas as pl
from jax.experimental.pallas import tpu as pltpu
from jax.sharding import PartitionSpec as P

ITERS = 3
AXES = ("gx", "gy", "gz")
F32 = jnp.float32
BF16 = jnp.bfloat16
MESH = pl.DeviceIdType.MESH


def up_to(value, step):
    return -(-value // step) * step


def mm(a, b, ca=1, cb=0):
    return lax.dot_general(a, b, (((ca,), (cb,)), ((), ())), preferred_element_type=F32)


def mmf(a, b, ca=1, cb=0):
    return lax.dot_general(
        a, b, (((ca,), (cb,)), ((), ())), precision=lax.Precision.HIGHEST, preferred_element_type=F32
    )


def split(x):
    hi = x.astype(BF16)
    return hi, (x - hi.astype(F32)).astype(BF16)


def pair(x):
    hi, lo = split(x)
    return jnp.concatenate([hi, lo], axis=1), hi


def dot3(hi, lo, packed, xhi):
    wide = mm(hi, packed)
    width = xhi.shape[1]
    return wide[:, :width] + wide[:, width:] + mm(lo, xhi)


def colsum(x):
    return jnp.sum(x, axis=0, keepdims=True)


def kernel(
    sizes,
    disp, small, flex, bmap, cnt, traces, dirs, images, curv,
    lam, w,
    perm, a_hi, a_lo, m_hi, m_lo, xd_hi, xd_lo, z_hi, z_lo, tm, t_hi, t_lo,
    g_src, g_dst, nm_src, nm_dst, hbuf, fbuf, ybuf, rs_src, rs_dst, bc_src, bc_dst,
    pbuf, qbuf, vbuf,
    g_ss, g_rs, nm_ss, nm_rs, f_ss, f_rs, rs_ss, rs_rs, bc_ss, bc_rs,
):
    nx, ny, nz = sizes
    n = nx * ny * nz
    slots, face, rhs = disp.shape
    nb = slots * face
    stored = dirs.shape[0]
    modes = traces.shape[0]
    mp = tm.shape[0]
    npad = n * mp
    koff = up_to(stored, 8)
    kw = xd_hi.shape[1]
    chunk = rs_src.shape[1]
    cx, cy, cz = (lax.axis_index(a) for a in AXES)
    me = (cx * ny + cy) * nz + cz

    def coords(e):
        return (e // (ny * nz), (e // nz) % ny, e % nz)

    def neighbour(slot):
        c = [cx, cy, cz]
        a = slot // 2
        step = sizes[a] - 1 if slot % 2 == 0 else 1
        c[a] = lax.rem(c[a] + step, sizes[a])
        return tuple(c)

    def linear(c):
        return (c[0] * ny + c[1]) * nz + c[2]

    def sl(s):
        return slice(s * face, (s + 1) * face)

    def peers(body):
        def step(r, carry):
            body(lax.rem(me + r, n))
            return carry
        lax.fori_loop(1, n, step, 0)

    def to_peer(src, dst, ss, rs, e):
        return pltpu.make_async_remote_copy(
            src_ref=src, dst_ref=dst.at[me], send_sem=ss.at[e], recv_sem=rs.at[me],
            device_id=coords(e), device_id_type=MESH)

    def from_peer(src, dst, ss, rs, e):
        return pltpu.make_async_remote_copy(
            src_ref=src, dst_ref=dst.at[e], send_sem=ss.at[e], recv_sem=rs.at[e],
            device_id=coords(e), device_id_type=MESH)

    def to_face(src, dst, ss, rs, s):
        return pltpu.make_async_remote_copy(
            src_ref=src.at[s], dst_ref=dst.at[s ^ 1], send_sem=ss.at[s], recv_sem=rs.at[s ^ 1],
            device_id=neighbour(s), device_id_type=MESH)

    barrier = pltpu.get_barrier_semaphore()
    peers(lambda e: pl.semaphore_signal(barrier, inc=1, device_id=coords(e), device_id_type=MESH))

    signs = [-1.0, 1.0] * (slots // 2)
    present = (lax.broadcasted_iota(jnp.int32, (modes, face), 0) < cnt[0]).astype(F32)
    tm[...] = jnp.zeros_like(tm)
    nm_src[...] = jnp.zeros_like(nm_src)
    g_src[:, npad + rhs:] = jnp.zeros((mp, kw), F32)
    g_src[:, :npad + rhs] = small[...]
    kz = jnp.zeros((mp, koff), F32)
    kd = jnp.zeros((mp, koff), F32)
    zero_rows = jnp.zeros((koff - stored, face), F32)
    for s in range(slots):
        block = traces[:, s, :] * present * signs[s]
        tm[0:modes, sl(s)] = block
        nm_src[s, 0:modes, :] = block
        full = nm_src[s]
        z = images[:, s, :]
        d = dirs[:, s, :]
        if koff > stored:
            z = jnp.concatenate([z, zero_rows], axis=0)
            d = jnp.concatenate([d, zero_rows], axis=0)
        zh, zl = split(z)
        z_hi[:, sl(s)] = zh
        z_lo[:, sl(s)] = zl
        kz = kz + mmf(full, z, 1, 1)
        kd = kd + mmf(full, d, 1, 1)
        parts = [jnp.zeros((koff, face), F32), d]
        if kw > 2 * koff:
            parts.append(jnp.zeros((kw - 2 * koff, face), F32))
        dt = jnp.concatenate(parts, axis=0).T
        dh, dl = split(dt)
        xd_hi[sl(s), :] = dh
        xd_lo[sl(s), :] = dl
    th, tl = split(tm[...])
    t_hi[...] = th
    t_lo[...] = tl
    g_src[:, npad + rhs:npad + rhs + koff] = kz
    g_src[:, npad + rhs + koff:npad + rhs + 2 * koff] = kd
    g_dst[me] = g_src[...]

    pl.semaphore_wait(barrier, n - 1)
    peers(lambda e: to_peer(g_src, g_dst, g_ss, g_rs, e).start())
    for s in range(slots):
        to_face(nm_src, nm_dst, nm_ss, nm_rs, s).start()

    for s in range(slots):
        rows = lax.broadcasted_iota(jnp.int32, (face, nb), 0) + s * face
        perm[sl(s), :] = jnp.where(rows == bmap[...], signs[s], 0.0).astype(BF16)
    fhi, flo = split(flex[...])

    for s in range(slots):
        p = perm[sl(s), :]
        a_hi[sl(s), :] = mm(mm(p, fhi).astype(BF16), perm[...], 1, 1).astype(BF16)
        a_lo[sl(s), :] = mm(mm(p, flo).astype(BF16), perm[...], 1, 1).astype(BF16)

    for s in range(slots):
        to_face(nm_src, nm_dst, nm_ss, nm_rs, s).wait()
    peers(lambda e: from_peer(g_src, g_dst, g_ss, g_rs, e).wait())

    cg = g_dst[:, :, 0:npad].reshape(npad, npad)
    load = g_dst[:, :, npad:npad + rhs].reshape(npad, rhs)
    kg = g_dst[:, :, npad + rhs:].reshape(npad, kw)
    for s in range(slots):
        own = mmf(nm_src[s], g_src[:, 0:npad], 0, 0)
        other = mmf(nm_dst[s], g_dst[linear(neighbour(s))][:, 0:npad], 0, 0)
        mh, ml = split(own + other)
        m_hi[sl(s), :] = mh
        m_lo[sl(s), :] = ml
    mh, ml = split(mmf(kg, cg, 0, 0))
    m_hi[nb:nb + kw, :] = mh
    m_lo[nb:nb + kw, :] = ml
    mh, ml = split(cg)
    m_hi[nb + kw:, :] = mh
    m_lo[nb + kw:, :] = ml
    xh, xl = split(mmf(cg, kg))
    xd_hi[nb:, :] = xh
    xd_lo[nb:, :] = xl

    lp, lh = pair(load)
    lam0 = dot3(m_hi[0:nb, :], m_lo[0:nb, :], lp, lh)
    for s in range(slots):
        lam[s] = lam0[sl(s), :]
    bc_src[...] = jnp.zeros_like(bc_src)
    rs_src[...] = jnp.zeros_like(rs_src)

    def advance(field, extras, first):
        fp, fh = pair(field)
        acc = [[] for _ in extras]
        for s in range(slots):
            h = dot3(a_hi[sl(s), :], a_lo[sl(s), :], fp, fh)
            if first:
                h = disp[s] * signs[s] - h
            hbuf[s] = h
            to_face(hbuf, fbuf, f_ss, f_rs, s).start()
        hall = hbuf[...].reshape(nb, rhs)
        hp, hh = pair(hall)
        zh = dot3(z_hi[...], z_lo[...], hp, hh)
        rows = [zh]
        count = koff
        for u, v in extras:
            rows.append(colsum(u * (hall if v is None else v)))
            count += 1
        if chunk * n > count:
            rows.append(jnp.zeros((chunk * n - count, rhs), F32))
        full = jnp.concatenate(rows, axis=0)
        for j in range(chunk):
            rs_src[:, j, :] = full[j * n:(j + 1) * n]
        rs_dst[me] = rs_src[me]
        peers(lambda e: to_peer(rs_src.at[e], rs_dst, rs_ss, rs_rs, e).start())
        for s in range(slots):
            to_face(hbuf, fbuf, f_ss, f_rs, s).wait()
        y = hall + fbuf[...].reshape(nb, rhs)
        ybuf[...] = y
        yy = colsum(hall * y)
        yp, yh = pair(y)
        c_own = dot3(t_hi[...], t_lo[...], yp, yh)
        bc_src[0:mp, :] = c_own
        bc_src[mp:mp + 1, :] = yy
        peers(lambda e: from_peer(rs_src.at[e], rs_dst, rs_ss, rs_rs, e).wait())
        bc_src[mp + 1:mp + 1 + chunk, :] = jnp.sum(rs_dst[...], axis=0)
        bc_dst[me] = bc_src[...]
        peers(lambda e: to_peer(bc_src, bc_dst, bc_ss, bc_rs, e).start())
        peers(lambda e: from_peer(bc_src, bc_dst, bc_ss, bc_rs, e).wait())
        got = bc_dst[...]
        c = got[:, 0:mp, :].reshape(npad, rhs)
        yy = jnp.sum(got[:, mp, :], axis=0, keepdims=True)
        totals = jnp.concatenate([got[:, mp + 1 + j, :] for j in range(chunk)], axis=0)
        cp, ch = pair(c)
        res = dot3(m_hi[...], m_lo[...], cp, ch)
        image = ybuf[...] - res[0:nb]
        zq = totals[0:koff] - res[nb:nb + koff]
        alpha = res[nb + kw:]
        ex = [totals[koff + i:koff + i + 1] for i in range(len(extras))]
        return image, zq, ex, yy, c, alpha

    image, zw, _, _, _, _ = advance(lam0, [], True)
    w_now = image
    curve_inv = 1.0 / curv[...]
    qw = []
    curves = []
    for k in range(ITERS):
        beta = zw * curve_inv
        parts = [jnp.zeros((koff, rhs), F32), beta]
        if kw > 2 * koff:
            parts.append(jnp.zeros((kw - 2 * koff, rhs), F32))
        bp, bh = pair(jnp.concatenate(parts, axis=0))
        sub = dot3(xd_hi[...], xd_lo[...], bp, bh)
        p = w_now - sub[0:nb]
        v = -sub[nb:]
        for j in range(k):
            gamma = qw[j] / curves[j]
            p = p - pbuf[j] * gamma
            v = v - vbuf[j] * gamma
        half = (lax.broadcasted_iota(jnp.int32, (nb, rhs), 0) // face) % 2
        extras = [(p, None), (w_now, None), (jnp.where(half == 1, p, 0.0), w_now)]
        extras += [(qbuf[j], None) for j in range(k)]
        image, zq, ex, yy, c, alpha = advance(p, extras, False)
        pq = ex[0] - colsum(v * c)
        rate = ex[2] / pq
        plain = rate * p
        for s in range(slots):
            lam[s] = lam[s] + plain[sl(s), :]
        if k + 1 < ITERS:
            pbuf[k] = p
            qbuf[k] = image
            vbuf[k] = v
            curves.append(pq)
            qw = [qw[j] - rate * ex[3 + j] for j in range(k)]
            qw.append(ex[1] - rate * (yy - colsum(c * alpha)))
            zw = zw - rate * zq
        w_now = w_now - rate * image
    for s in range(slots):
        w[s] = w_now[sl(s), :]


def per_device(sizes, local_displacement, coarse_load, flexibility, block_map, mode_counts,
               mode_traces, coarse_rows, stored_dirs, stored_images, stored_curv):
    n = sizes[0] * sizes[1] * sizes[2]
    disp = local_displacement[0, 0, 0]
    slots, face, rhs = disp.shape
    nb = slots * face
    traces = mode_traces[0, 0, 0]
    modes = traces.shape[0]
    stored = stored_dirs.shape[3]
    mp = up_to(modes, 8)
    npad = n * mp
    koff = up_to(stored, 8)
    kw = up_to(2 * koff, 128)
    chunk = -(-(koff + 3 + ITERS) // n)
    rows = jnp.pad(coarse_rows[0, 0, 0].reshape(modes, n, modes),
                   ((0, mp - modes), (0, 0), (0, mp - modes))).reshape(mp, npad)
    small = jnp.concatenate([rows, jnp.pad(coarse_load[0, 0, 0], ((0, mp - modes), (0, 0)))], axis=1)
    curv = jnp.pad(stored_curv, (0, koff - stored), constant_values=1.0)[:, None]
    width = npad + rhs + kw
    brow = up_to(mp + 1 + chunk, 8)
    vm = pl.BlockSpec(memory_space=pltpu.VMEM)
    sem = pltpu.SemaphoreType.DMA
    out = jax.ShapeDtypeStruct((slots, face, rhs), F32)
    lam, resid = pl.pallas_call(
        functools.partial(kernel, sizes),
        out_shape=(out, out),
        in_specs=[vm, vm, vm, vm, pl.BlockSpec(memory_space=pltpu.SMEM), vm, vm, vm, vm],
        out_specs=(vm, vm),
        scratch_shapes=[
            pltpu.VMEM((nb, nb), BF16),
            pltpu.VMEM((nb, nb), BF16), pltpu.VMEM((nb, nb), BF16),
            pltpu.VMEM((nb + kw + npad, npad), BF16), pltpu.VMEM((nb + kw + npad, npad), BF16),
            pltpu.VMEM((nb + npad, kw), BF16), pltpu.VMEM((nb + npad, kw), BF16),
            pltpu.VMEM((koff, nb), BF16), pltpu.VMEM((koff, nb), BF16),
            pltpu.VMEM((mp, nb), F32), pltpu.VMEM((mp, nb), BF16), pltpu.VMEM((mp, nb), BF16),
            pltpu.VMEM((mp, width), F32), pltpu.VMEM((n, mp, width), F32),
            pltpu.VMEM((slots, mp, face), F32), pltpu.VMEM((slots, mp, face), F32),
            pltpu.VMEM((slots, face, rhs), F32), pltpu.VMEM((slots, face, rhs), F32),
            pltpu.VMEM((nb, rhs), F32),
            pltpu.VMEM((n, chunk, rhs), F32), pltpu.VMEM((n, chunk, rhs), F32),
            pltpu.VMEM((brow, rhs), F32), pltpu.VMEM((n, brow, rhs), F32),
            pltpu.VMEM((ITERS - 1, nb, rhs), F32), pltpu.VMEM((ITERS - 1, nb, rhs), F32),
            pltpu.VMEM((ITERS - 1, npad, rhs), F32),
            sem((n,)), sem((n,)), sem((slots,)), sem((slots,)), sem((slots,)), sem((slots,)),
            sem((n,)), sem((n,)), sem((n,)), sem((n,)),
        ],
        compiler_params=pltpu.CompilerParams(
            collective_id=0, has_side_effects=True, vmem_limit_bytes=67043328),
    )(disp, small, flexibility[0, 0, 0], block_map[0, 0], mode_counts[0, 0], traces,
      stored_dirs[0, 0, 0], stored_images[0, 0, 0], curv)
    return lam[None, None, None], resid[None, None, None]


def extended(x, sides, width):
    for axis, dim in sides:
        peers, length = (lax.axis_size(axis), x.shape[dim])
        up = [(i, (i + 1) % peers) for i in range(peers)]
        down = [(j, i) for i, j in up]
        last = lax.slice_in_dim(x, length - width, length, axis=dim)
        initial = lax.slice_in_dim(x, 0, width, axis=dim)
        before = lax.ppermute(last, axis, up)
        after = lax.ppermute(initial, axis, down)
        x = jnp.concatenate([before, x, after], axis=dim)
    return x


def assemble(field):
    padded_x = extended(field[0:2], (("gx", 0),), 1)
    padded_y = extended(field[2:4], (("gy", 0),), 1)
    padded_z = extended(field[4:6], (("gz", 0),), 1)
    return jnp.stack(
        [
            field[0] + padded_x[0],
            field[1] + padded_x[3],
            field[2] + padded_y[0],
            field[3] + padded_y[3],
            field[4] + padded_z[0],
            field[5] + padded_z[3],
        ]
    )


def plus_inner(first, second):
    return jnp.sum(first[1::2] * second[1::2], axis=(0, 1))


def stored_inner(store, field):
    return jnp.einsum("isf,sfr->ir", store[:, 1::2], field[1::2], precision=lax.Precision.HIGHEST)


def coarse_solve(loads, rows):
    return jnp.dot(
        rows, lax.all_gather(loads, ("gx", "gy", "gz"), axis=0, tiled=True), precision=lax.Precision.HIGHEST
    )


def per_device_plain(
    local_displacement,
    coarse_load,
    flexibility,
    block_map,
    mode_counts,
    mode_traces,
    coarse_rows,
    stored_dirs,
    stored_images,
    stored_curv,
):
    displacement = local_displacement[0, 0, 0]
    loads = coarse_load[0, 0, 0]
    flex = flexibility[0, 0, 0]
    mapping = block_map[0, 0, 0]
    rows = coarse_rows[0, 0, 0]
    dirs_store = stored_dirs[0, 0, 0]
    images_store = stored_images[0, 0, 0]
    signs = jnp.array((-1.0, 1.0, -1.0, 1.0, -1.0, 1.0), jnp.float32)
    field_signs = signs[:, None, None]
    nmodes = mode_traces.shape[3]
    present = (jnp.arange(nmodes, dtype=jnp.int32) < mode_counts[0, 0, 0]).astype(jnp.float32)
    signed = mode_traces[0, 0, 0] * present[:, None, None] * signs[None, :, None]
    size_nb = flex.shape[0]
    inverse = jnp.zeros((size_nb,), jnp.int32).at[mapping].set(jnp.arange(size_nb, dtype=jnp.int32))
    flex_face = jnp.take(jnp.take(flex, inverse, axis=0), inverse, axis=1)
    layout = displacement.shape

    def operate(field):
        flat = (field_signs * field).reshape(size_nb, layout[2])
        return jnp.dot(flex_face, flat, precision=lax.Precision.HIGHEST).reshape(layout)

    def graph(alpha):
        return assemble(jnp.einsum("msf,mr->sfr", signed, alpha, precision=lax.Precision.HIGHEST))

    def project(field):
        partial_loads = jnp.einsum("msf,sfr->mr", signed, field, precision=lax.Precision.HIGHEST)
        return field - graph(coarse_solve(partial_loads, rows))

    lam = graph(coarse_solve(loads, rows))
    resid = project(assemble(field_signs * (displacement - operate(lam))))
    directions, images, curves = ([], [], [])
    for step in range(ITERS):
        local_rows = stored_inner(images_store, resid)
        if images:
            own_rows = jnp.stack([plus_inner(images[index], resid) for index in range(len(images))])
            local_rows = jnp.concatenate([local_rows, own_rows], axis=0)
        totals = lax.psum(local_rows, ("gx", "gy", "gz"))
        beta = totals[:stored_curv.shape[0]] / stored_curv[:, None]
        direction = resid - jnp.einsum("isf,ir->sfr", dirs_store, beta, precision=lax.Precision.HIGHEST)
        for index in range(len(directions)):
            direction = direction - directions[index] * (totals[stored_curv.shape[0] + index] / curves[index])
        image_now = project(assemble(field_signs * operate(direction)))
        pair = lax.psum(
            jnp.stack([plus_inner(direction, image_now), plus_inner(direction, resid)]),
            ("gx", "gy", "gz"),
        )
        rate = pair[1] / pair[0]
        lam = lam + rate * direction
        resid = resid - rate * image_now
        directions.append(direction)
        images.append(image_now)
        curves.append(pair[0])
    return (lam[None, None, None], resid[None, None, None])


def solution(mesh):
    sizes = tuple(mesh.shape[a] for a in AXES)
    grid = P(*AXES)

    def program(*args):
        coarse = sizes[0] * sizes[1] * sizes[2] * up_to(args[5].shape[3], 8)
        one = functools.partial(per_device, sizes) if coarse <= 512 else per_device_plain
        return jax.shard_map(
            one,
            mesh=mesh,
            in_specs=(grid,) * 9 + (P(),),
            out_specs=(grid, grid),
            check_vma=False,
        )(*args)

    return program
```

```python
import functools

import jax
import jax.numpy as jnp
from jax import lax
from jax.experimental import pallas as pl
from jax.experimental.pallas import tpu as pltpu
from jax.sharding import PartitionSpec as P

ITERS = 3
AXES = ("gx", "gy", "gz")
F32 = jnp.float32
BF16 = jnp.bfloat16
MESH = pl.DeviceIdType.MESH


def up_to(value, step):
    return -(-value // step) * step


def mm(a, b, ca=1, cb=0):
    return lax.dot_general(a, b, (((ca,), (cb,)), ((), ())), preferred_element_type=F32)


def mmf(a, b, ca=1, cb=0):
    return lax.dot_general(
        a, b, (((ca,), (cb,)), ((), ())), precision=lax.Precision.HIGHEST, preferred_element_type=F32
    )


def split(x):
    hi = x.astype(BF16)
    return hi, (x - hi.astype(F32)).astype(BF16)


def pair(x):
    hi, lo = split(x)
    return jnp.concatenate([hi, lo], axis=1), hi


def dot3(hi, lo, packed, xhi):
    wide = mm(hi, packed)
    width = xhi.shape[1]
    return wide[:, :width] + wide[:, width:] + mm(lo, xhi)


def colsum(x):
    return jnp.sum(x, axis=0, keepdims=True)


def kernel(
    sizes,
    disp, rows_in, load_in, flex, bmap, cnt, traces, dirs, images, curv,
    lam, w,
    perm, a_hi, a_lo, m_hi, m_lo, xd_hi, xd_lo, z_hi, z_lo, tm, t_hi, t_lo,
    g_src, g_dst, l_src, l_dst, nm_src, nm_dst, hbuf, fbuf, ybuf, rs_src, rs_dst, bc_src, bc_dst,
    pbuf, qbuf, vbuf,
    g_ss, g_rs, l_ss, l_rs, nm_ss, nm_rs, f_ss, f_rs, rs_ss, rs_rs, bc_ss, bc_rs,
):
    nx, ny, nz = sizes
    n = nx * ny * nz
    slots, face, rhs = disp.shape
    nb = slots * face
    stored = dirs.shape[1]
    modes = load_in.shape[0]
    mp = tm.shape[0]
    npad = n * mp
    koff = up_to(stored, 8)
    kw = xd_hi.shape[1]
    chunk = rs_src.shape[1]
    cx, cy, cz = (lax.axis_index(a) for a in AXES)
    me = (cx * ny + cy) * nz + cz

    here = (cx, cy, cz)
    plus = [[lax.rem(c + d, size) for d in range(size)] for c, size in zip(here, sizes)]
    minus = [[lax.rem(c + size - d, size) for d in range(size)] for c, size in zip(here, sizes)]
    offsets = [(i, j, l) for i in range(nx) for j in range(ny) for l in range(nz)][1:]
    offsets.sort(key=lambda o: -sum(min(d, size - d) for d, size in zip(o, sizes)))

    def target(o):
        return tuple(plus[a][o[a]] for a in range(3))

    def origin(o):
        return tuple(minus[a][o[a]] for a in range(3))

    def neighbour(slot):
        c = [cx, cy, cz]
        a = slot // 2
        step = sizes[a] - 1 if slot % 2 == 0 else 1
        c[a] = lax.rem(c[a] + step, sizes[a])
        return tuple(c)

    def linear(c):
        return (c[0] * ny + c[1]) * nz + c[2]

    def sl(s):
        return slice(s * face, (s + 1) * face)

    def peers(body):
        for r, o in enumerate(offsets):
            body(r, o)

    def to_peer(src, dst, ss, rs, r, o):
        return pltpu.make_async_remote_copy(
            src_ref=src, dst_ref=dst, send_sem=ss.at[r], recv_sem=rs.at[r],
            device_id=target(o), device_id_type=MESH)

    def to_face(src, dst, ss, rs, s):
        return pltpu.make_async_remote_copy(
            src_ref=src.at[s], dst_ref=dst.at[s ^ 1], send_sem=ss.at[s], recv_sem=rs.at[s ^ 1],
            device_id=neighbour(s), device_id_type=MESH)

    barrier = pltpu.get_barrier_semaphore()
    peers(lambda r, o: pl.semaphore_signal(
        barrier, inc=1, device_id=target(o), device_id_type=MESH))

    signs = [-1.0, 1.0] * (slots // 2)
    present = (lax.broadcasted_iota(jnp.int32, (modes, face), 0) < cnt[...]).astype(F32)
    tm[...] = jnp.zeros_like(tm)
    nm_src[...] = jnp.zeros_like(nm_src)
    g_src[...] = jnp.zeros_like(g_src)
    l_src[...] = jnp.zeros_like(l_src)
    l_src[0:modes, :] = load_in[:, 0, :]
    wide = lax.broadcasted_iota(jnp.int32, (n * modes, npad), 1)
    tall = lax.broadcasted_iota(jnp.int32, (n * modes, npad), 0)
    spread = (wide // mp * modes + wide % mp == tall) & (wide % mp < modes)
    g_src[0:modes, 0:npad] = mmf(rows_in[:, 0, :], spread.astype(F32))
    kz = jnp.zeros((mp, koff), F32)
    kd = jnp.zeros((mp, koff), F32)
    zero_rows = jnp.zeros((koff - stored, face), F32)
    for s in range(slots):
        block = jnp.concatenate([traces[m * slots + s] for m in range(modes)], axis=0)
        block = block * present * signs[s]
        tm[0:modes, sl(s)] = block
        nm_src[s, 0:modes, npad:] = block
        nm_src[s, :, 0:npad] = g_src[:, 0:npad]
        full = nm_src[s, :, npad:]
        z = images[s]
        d = dirs[s]
        if koff > stored:
            z = jnp.concatenate([z, zero_rows], axis=0)
            d = jnp.concatenate([d, zero_rows], axis=0)
        zh, zl = split(z)
        z_hi[:, sl(s)] = zh
        z_lo[:, sl(s)] = zl
        kz = kz + mmf(full, z, 1, 1)
        kd = kd + mmf(full, d, 1, 1)
        parts = [jnp.zeros((koff, face), F32), d]
        if kw > 2 * koff:
            parts.append(jnp.zeros((kw - 2 * koff, face), F32))
        dt = jnp.concatenate(parts, axis=0).T
        dh, dl = split(dt)
        xd_hi[sl(s), :] = dh
        xd_lo[sl(s), :] = dl
    th, tl = split(tm[...])
    t_hi[...] = th
    t_lo[...] = tl
    g_src[:, npad:npad + koff] = kz
    g_src[:, npad + koff:npad + 2 * koff] = kd
    g_dst[me] = g_src[...]
    l_dst[me] = l_src[...]
    for s in range(slots):
        rows = lax.broadcasted_iota(jnp.int32, (face, nb), 0) + s * face
        perm[sl(s), :] = jnp.where(rows == bmap[...], signs[s], 0.0).astype(BF16)

    pl.semaphore_wait(barrier, n - 1)
    peers(lambda r, o: to_peer(l_src, l_dst.at[me], l_ss, l_rs, r, o).start())
    for s in range(slots):
        to_face(nm_src, nm_dst, nm_ss, nm_rs, s).start()
    peers(lambda r, o: to_peer(g_src, g_dst.at[me], g_ss, g_rs, r, o).start())

    fhi, flo = split(flex[...])

    for s in range(slots):
        p = perm[sl(s), :]
        a_hi[sl(s), :] = mm(mm(p, fhi).astype(BF16), perm[...], 1, 1).astype(BF16)
        a_lo[sl(s), :] = mm(mm(p, flo).astype(BF16), perm[...], 1, 1).astype(BF16)

    for s in range(slots):
        to_face(nm_src, nm_dst, nm_ss, nm_rs, s).wait()
    peers(lambda r, o: to_peer(l_src, l_dst.at[linear(origin(o))], l_ss, l_rs, r, o).wait())

    load = l_dst[...].reshape(npad, rhs)
    for s in range(slots):
        own = mmf(nm_src[s, :, npad:], g_src[:, 0:npad], 0, 0)
        other = mmf(nm_dst[s, :, npad:], nm_dst[s, :, 0:npad], 0, 0)
        mh, ml = split(own + other)
        m_hi[sl(s), :] = mh
        m_lo[sl(s), :] = ml

    def finish_setup():
        peers(lambda r, o: to_peer(g_src, g_dst.at[linear(origin(o))], g_ss, g_rs, r, o).wait())
        cg = g_dst[:, :, 0:npad].reshape(npad, npad)
        kg = g_dst[:, :, npad:].reshape(npad, kw)
        mh, ml = split(mmf(kg, cg, 0, 0))
        m_hi[nb:nb + kw, :] = mh
        m_lo[nb:nb + kw, :] = ml
        mh, ml = split(cg)
        m_hi[nb + kw:, :] = mh
        m_lo[nb + kw:, :] = ml
        xh, xl = split(mmf(cg, kg))
        xd_hi[nb:, :] = xh
        xd_lo[nb:, :] = xl

    lp, lh = pair(load)
    lam0 = dot3(m_hi[0:nb, :], m_lo[0:nb, :], lp, lh)
    for s in range(slots):
        lam[s] = lam0[sl(s), :]
    bc_src[...] = jnp.zeros_like(bc_src)
    rs_src[...] = jnp.zeros_like(rs_src)

    def advance(field, extras, first, last=False):
        fp, fh = pair(field)
        for s in range(slots):
            h = dot3(a_hi[sl(s), :], a_lo[sl(s), :], fp, fh)
            if first:
                h = disp[s] * signs[s] - h
            hbuf[s] = h
            to_face(hbuf, fbuf, f_ss, f_rs, s).start()
        hall = hbuf[...].reshape(nb, rhs)
        hp, hh = pair(hall)
        zh = dot3(z_hi[...], z_lo[...], hp, hh)
        rows = [zh]
        count = koff
        for u, v in extras:
            rows.append(colsum(u * (hall if v is None else v)))
            count += 1
        if chunk * n > count:
            rows.append(jnp.zeros((chunk * n - count, rhs), F32))
        full = jnp.concatenate(rows, axis=0)
        for j in range(chunk):
            rs_src[:, j, :] = full[j * n:(j + 1) * n]
        rs_dst[me] = rs_src[me]
        peers(lambda r, o: to_peer(
            rs_src.at[linear(target(o))], rs_dst.at[me], rs_ss, rs_rs, r, o).start())
        if first:
            finish_setup()
        for s in range(slots):
            to_face(hbuf, fbuf, f_ss, f_rs, s).wait()
        y = hall + fbuf[...].reshape(nb, rhs)
        ybuf[...] = y
        yp, yh = pair(y)
        c_own = dot3(t_hi[...], t_lo[...], yp, yh)
        bc_src[0:mp, :] = c_own
        squares = not (first or last)
        fits = modes + chunk <= mp
        if squares:
            bc_src[mp:mp + 1, :] = colsum(hall * y)
        at = modes if fits else mp + 1
        used = mp + squares if fits else mp + 1 + chunk
        peers(lambda r, o: to_peer(
            rs_src.at[linear(target(o))], rs_dst.at[linear(origin(o))], rs_ss, rs_rs, r, o).wait())
        bc_src[at:at + chunk, :] = jnp.sum(rs_dst[...], axis=0)
        bc_dst[me] = bc_src[...]
        part = bc_src.at[0:used]
        peers(lambda r, o: to_peer(part, bc_dst.at[me, 0:used], bc_ss, bc_rs, r, o).start())
        peers(lambda r, o: to_peer(
            part, bc_dst.at[linear(origin(o)), 0:used], bc_ss, bc_rs, r, o).wait())
        c = bc_dst[:, 0:mp, :].reshape(npad, rhs)
        yy = jnp.sum(bc_dst[:, mp, :], axis=0, keepdims=True) if squares else None
        totals = jnp.concatenate([bc_dst[:, at + j, :] for j in range(chunk)], axis=0)
        cp, ch = pair(c)
        need = nb if last else nb + kw if first else nb + kw + npad
        res = dot3(m_hi[0:need, :], m_lo[0:need, :], cp, ch)
        image = ybuf[...] - res[0:nb]
        zq = None if last else totals[0:koff] - res[nb:nb + koff]
        alpha = res[nb + kw:] if squares else None
        ex = [totals[koff + i:koff + i + 1] for i in range(len(extras))]
        return image, zq, ex, yy, c, alpha

    image, zw, _, _, _, _ = advance(lam0, [], True)
    w_now = image
    square = (koff, koff)
    eye = lax.broadcasted_iota(jnp.int32, square, 0) == lax.broadcasted_iota(jnp.int32, square, 1)
    curve_inv = 1.0 / jnp.sum(jnp.where(eye, curv[...], 0.0), axis=1, keepdims=True)
    qw = []
    curves = []
    for k in range(ITERS):
        beta = zw * curve_inv
        parts = [jnp.zeros((koff, rhs), F32), beta]
        if kw > 2 * koff:
            parts.append(jnp.zeros((kw - 2 * koff, rhs), F32))
        bp, bh = pair(jnp.concatenate(parts, axis=0))
        sub = dot3(xd_hi[...], xd_lo[...], bp, bh)
        p = w_now - sub[0:nb]
        v = -sub[nb:]
        for j in range(k):
            gamma = qw[j] / curves[j]
            p = p - pbuf[j] * gamma
            v = v - vbuf[j] * gamma
        half = (lax.broadcasted_iota(jnp.int32, (nb, rhs), 0) // face) % 2
        extras = [(p, None), (w_now, None), (jnp.where(half == 1, p, 0.0), w_now)]
        extras += [(qbuf[j], None) for j in range(k)]
        image, zq, ex, yy, c, alpha = advance(p, extras, False, k + 1 == ITERS)
        pq = ex[0] - colsum(v * c)
        rate = ex[2] / pq
        plain = rate * p
        for s in range(slots):
            lam[s] = lam[s] + plain[sl(s), :]
        if k + 1 < ITERS:
            pbuf[k] = p
            qbuf[k] = image
            vbuf[k] = v
            curves.append(pq)
            qw = [qw[j] - rate * ex[3 + j] for j in range(k)]
            qw.append(ex[1] - rate * (yy - colsum(c * alpha)))
            zw = zw - rate * zq
        w_now = w_now - rate * image
    for s in range(slots):
        w[s] = w_now[sl(s), :]


def per_device(sizes, local_displacement, coarse_load, flexibility, block_map, mode_counts,
               mode_traces, coarse_rows, stored_dirs, stored_images, stored_curv):
    n = sizes[0] * sizes[1] * sizes[2]
    disp = local_displacement[0, 0, 0]
    slots, face, rhs = disp.shape
    nb = slots * face
    modes = mode_traces.shape[3]
    traces = mode_traces.reshape(modes * slots, 1, face)
    stored = stored_dirs.shape[3]
    mp = up_to(modes, 8)
    npad = n * mp
    koff = up_to(stored, 8)
    kw = up_to(2 * koff, 128)
    chunk = -(-(koff + 3 + ITERS) // n)
    curv = jnp.pad(stored_curv, (0, koff - stored), constant_values=1.0)[None]
    width = npad + kw
    brow = up_to(mp + 1 + chunk, 8)
    vm = pl.BlockSpec(memory_space=pltpu.VMEM)
    sem = pltpu.SemaphoreType.DMA
    out = jax.ShapeDtypeStruct((slots, face, rhs), F32)
    lam, resid = pl.pallas_call(
        functools.partial(kernel, sizes),
        out_shape=(out, out),
        in_specs=[vm] * 10,
        out_specs=(vm, vm),
        scratch_shapes=[
            pltpu.VMEM((nb, nb), BF16),
            pltpu.VMEM((nb, nb), BF16), pltpu.VMEM((nb, nb), BF16),
            pltpu.VMEM((nb + kw + npad, npad), BF16), pltpu.VMEM((nb + kw + npad, npad), BF16),
            pltpu.VMEM((nb + npad, kw), BF16), pltpu.VMEM((nb + npad, kw), BF16),
            pltpu.VMEM((koff, nb), BF16), pltpu.VMEM((koff, nb), BF16),
            pltpu.VMEM((mp, nb), F32), pltpu.VMEM((mp, nb), BF16), pltpu.VMEM((mp, nb), BF16),
            pltpu.VMEM((mp, width), F32), pltpu.VMEM((n, mp, width), F32),
            pltpu.VMEM((mp, rhs), F32), pltpu.VMEM((n, mp, rhs), F32),
            pltpu.VMEM((slots, mp, npad + face), F32), pltpu.VMEM((slots, mp, npad + face), F32),
            pltpu.VMEM((slots, face, rhs), F32), pltpu.VMEM((slots, face, rhs), F32),
            pltpu.VMEM((nb, rhs), F32),
            pltpu.VMEM((n, chunk, rhs), F32), pltpu.VMEM((n, chunk, rhs), F32),
            pltpu.VMEM((brow, rhs), F32), pltpu.VMEM((n, brow, rhs), F32),
            pltpu.VMEM((ITERS - 1, nb, rhs), F32), pltpu.VMEM((ITERS - 1, nb, rhs), F32),
            pltpu.VMEM((ITERS - 1, npad, rhs), F32),
            sem((n,)), sem((n,)), sem((n,)), sem((n,)), sem((slots,)), sem((slots,)), sem((slots,)), sem((slots,)),
            sem((n,)), sem((n,)), sem((n,)), sem((n,)),
        ],
        compiler_params=pltpu.CompilerParams(
            collective_id=0, has_side_effects=True, vmem_limit_bytes=67043328),
    )(disp, coarse_rows.reshape(modes, 1, n * modes), coarse_load.reshape(modes, 1, rhs),
      flexibility[0, 0, 0], block_map[0, 0], mode_counts[0], traces,
      jnp.swapaxes(stored_dirs[0, 0, 0], 0, 1), jnp.swapaxes(stored_images[0, 0, 0], 0, 1), curv)
    return lam[None, None, None], resid[None, None, None]


def extended(x, sides, width):
    for axis, dim in sides:
        peers, length = (lax.axis_size(axis), x.shape[dim])
        up = [(i, (i + 1) % peers) for i in range(peers)]
        down = [(j, i) for i, j in up]
        last = lax.slice_in_dim(x, length - width, length, axis=dim)
        initial = lax.slice_in_dim(x, 0, width, axis=dim)
        before = lax.ppermute(last, axis, up)
        after = lax.ppermute(initial, axis, down)
        x = jnp.concatenate([before, x, after], axis=dim)
    return x


def assemble(field):
    padded_x = extended(field[0:2], (("gx", 0),), 1)
    padded_y = extended(field[2:4], (("gy", 0),), 1)
    padded_z = extended(field[4:6], (("gz", 0),), 1)
    return jnp.stack(
        [
            field[0] + padded_x[0],
            field[1] + padded_x[3],
            field[2] + padded_y[0],
            field[3] + padded_y[3],
            field[4] + padded_z[0],
            field[5] + padded_z[3],
        ]
    )


def plus_inner(first, second):
    return jnp.sum(first[1::2] * second[1::2], axis=(0, 1))


def stored_inner(store, field):
    return jnp.einsum("isf,sfr->ir", store[:, 1::2], field[1::2], precision=lax.Precision.HIGHEST)


def coarse_solve(loads, rows):
    return jnp.dot(
        rows, lax.all_gather(loads, ("gx", "gy", "gz"), axis=0, tiled=True), precision=lax.Precision.HIGHEST
    )


def per_device_plain(
    local_displacement,
    coarse_load,
    flexibility,
    block_map,
    mode_counts,
    mode_traces,
    coarse_rows,
    stored_dirs,
    stored_images,
    stored_curv,
):
    displacement = local_displacement[0, 0, 0]
    loads = coarse_load[0, 0, 0]
    flex = flexibility[0, 0, 0]
    mapping = block_map[0, 0, 0]
    rows = coarse_rows[0, 0, 0]
    dirs_store = stored_dirs[0, 0, 0]
    images_store = stored_images[0, 0, 0]
    signs = jnp.array((-1.0, 1.0, -1.0, 1.0, -1.0, 1.0), jnp.float32)
    field_signs = signs[:, None, None]
    nmodes = mode_traces.shape[3]
    present = (jnp.arange(nmodes, dtype=jnp.int32) < mode_counts[0, 0, 0]).astype(jnp.float32)
    signed = mode_traces[0, 0, 0] * present[:, None, None] * signs[None, :, None]
    size_nb = flex.shape[0]
    inverse = jnp.zeros((size_nb,), jnp.int32).at[mapping].set(jnp.arange(size_nb, dtype=jnp.int32))
    flex_face = jnp.take(jnp.take(flex, inverse, axis=0), inverse, axis=1)
    layout = displacement.shape

    def operate(field):
        flat = (field_signs * field).reshape(size_nb, layout[2])
        return jnp.dot(flex_face, flat, precision=lax.Precision.HIGHEST).reshape(layout)

    def graph(alpha):
        return assemble(jnp.einsum("msf,mr->sfr", signed, alpha, precision=lax.Precision.HIGHEST))

    def project(field):
        partial_loads = jnp.einsum("msf,sfr->mr", signed, field, precision=lax.Precision.HIGHEST)
        return field - graph(coarse_solve(partial_loads, rows))

    lam = graph(coarse_solve(loads, rows))
    resid = project(assemble(field_signs * (displacement - operate(lam))))
    directions, images, curves = ([], [], [])
    for step in range(ITERS):
        local_rows = stored_inner(images_store, resid)
        if images:
            own_rows = jnp.stack([plus_inner(images[index], resid) for index in range(len(images))])
            local_rows = jnp.concatenate([local_rows, own_rows], axis=0)
        totals = lax.psum(local_rows, ("gx", "gy", "gz"))
        beta = totals[:stored_curv.shape[0]] / stored_curv[:, None]
        direction = resid - jnp.einsum("isf,ir->sfr", dirs_store, beta, precision=lax.Precision.HIGHEST)
        for index in range(len(directions)):
            direction = direction - directions[index] * (totals[stored_curv.shape[0] + index] / curves[index])
        image_now = project(assemble(field_signs * operate(direction)))
        pair = lax.psum(
            jnp.stack([plus_inner(direction, image_now), plus_inner(direction, resid)]),
            ("gx", "gy", "gz"),
        )
        rate = pair[1] / pair[0]
        lam = lam + rate * direction
        resid = resid - rate * image_now
        directions.append(direction)
        images.append(image_now)
        curves.append(pair[0])
    return (lam[None, None, None], resid[None, None, None])


def solution(mesh):
    sizes = tuple(mesh.shape[a] for a in AXES)
    grid = P(*AXES)

    def program(*args):
        coarse = sizes[0] * sizes[1] * sizes[2] * up_to(args[5].shape[3], 8)
        one = functools.partial(per_device, sizes) if coarse <= 512 else per_device_plain
        return jax.shard_map(
            one,
            mesh=mesh,
            in_specs=(grid,) * 9 + (P(),),
            out_specs=(grid, grid),
            check_vma=False,
        )(*args)

    return program
```
